32 devices in a mesh: freq: 32 (over z, y, x, core).
Axes of the slice: x: 2, y: 2, z: 4, core: 2. Of those that a mesh axis runs over, the one named last changes fastest.
Arguments:
- model_vis: bfloat16 [64, 8, 4096], P('freq'), may hold values from -6 to 6
- observed: float32 [64, 4096], P('freq'), may hold values from -48 to 48
- row_keep: int32 [64, 4096], P('freq'), may hold values 0 or 1
- station_one: int32 [4096], replicated, may hold values from 0 to 61, as said below
- station_two: int32 [4096], replicated, may hold values from 0 to 61
- smoothness: float32 [496], replicated, may hold values from 4 to 24576
Outputs:
- gains: float32 [64, 496], P('freq')
The draws below stay inside these ranges and needn't reach their ends.
Inputs may be any that keep to these rules, and one draw needn't show every extreme that they name: station_one and station_two differ in every row.
All inputs are finite; a program needn't handle non-finite values. No bound on the sum of `row_keep` on one device may be relied on, other than what follows from the above.
Results may differ from the reference program's by a relative error of at most 0.0003.
Values sent between devices are 32-bit elements; how exact they have to be, the bound alone decides.
A program may use at most 256 MiB of HBM per device.

```python
import math
import jax
import jax.numpy as jnp
from jax import lax

STATIONS = 62
DIRECTIONS = 8
ROWS = 4096
BLOCK = 496
CHANNELS = 64


def station_pairs(key):
    folded = jax.random.fold_in(key, 31)
    first_key, offset_key = jax.random.split(folded)
    leading = jax.random.randint(first_key, (ROWS,), 0, STATIONS, dtype=jnp.int32)
    offset = jax.random.randint(offset_key, (ROWS,), 1, STATIONS, dtype=jnp.int32)
    return (leading, (leading + offset) % STATIONS)


def draw_station_one(key, part):
    return station_pairs(key)[0]


def draw_station_two(key, part):
    return station_pairs(key)[1]


def draw_model_vis(key, part):
    folded = jax.random.fold_in(key, 53)
    value_key, pick_key = jax.random.split(folded)
    values = jax.random.truncated_normal(value_key, -6.0, 6.0, (CHANNELS, DIRECTIONS, ROWS), jnp.float32)
    faint_direction = jax.random.randint(pick_key, (), 0, DIRECTIONS, dtype=jnp.int32)
    channel_index = jnp.arange(CHANNELS, dtype=jnp.int32)
    direction_index = jnp.arange(DIRECTIONS, dtype=jnp.int32)
    faint = (channel_index[:, None] < CHANNELS // 2) & (direction_index[None, :] == faint_direction)
    factor = jnp.where(faint, 0.01, 1.0).astype(jnp.float32)
    return (values * factor[:, :, None]).astype(jnp.bfloat16)


def with_ends(array, own_key, smallest, top_value):
    shape = array.shape
    index_at = [jax.random.randint(jax.random.fold_in(own_key, axis), (), 0, shape[axis]) for axis in range(len(shape))]
    array = array.at[tuple(index_at)].set(smallest)
    longest = shape.index(max(shape))
    index_at[longest] = (index_at[longest] + 1) % shape[longest]
    return array.at[tuple(index_at)].set(top_value)


def block_levels(own_key, dims, cuts, low, largest):
    loudness = 1.0
    for dim, blocks in cuts:
        heights = jax.random.uniform(jax.random.fold_in(jax.random.fold_in(own_key, 6), dim), (blocks,), jnp.float32, low / len(cuts), largest / len(cuts))
        loudness = loudness * jnp.repeat(jnp.exp(heights), dims[dim] // blocks).reshape((-1,) + (1,) * (len(dims) - 1 - dim))
    return loudness


def centred(stream_key, dims, scale, limit, shards=(), held_as=jnp.bfloat16):
    array = scale * jax.random.normal(stream_key, dims, jnp.float32)
    if shards:
        array = array * block_levels(stream_key, dims, shards, -0.22, 0.18)
    return jnp.clip(array, -limit, limit).astype(held_as)


def setup_inputs(seed: int = 0) -> dict:
    seeds = jax.random.split(jax.random.key(seed), 7)
    return {
        "model_vis": draw_model_vis(jax.random.fold_in(seeds[6], 71), 0),
        "observed": centred(seeds[1], (CHANNELS, ROWS), 8.0, 48.0, ((0, 32),), jnp.float32),
        "row_keep": with_ends((jax.random.randint(seeds[2], (CHANNELS, ROWS), 0, 4) < 3).astype(jnp.int32), jax.random.fold_in(seeds[2], 1), 0, 1),
        "station_one": draw_station_one(jax.random.fold_in(seeds[6], 71), 0),
        "station_two": draw_station_two(jax.random.fold_in(seeds[6], 71), 0),
        "smoothness": jnp.clip(jnp.exp(jax.random.uniform(seeds[5], (BLOCK,), jnp.float32, math.log(4.0), math.log(24576.0))), 4.0, 24576.0),
    }


ridge_weight = 1.0

def product(left, right):
    return jnp.dot(left, right, precision=lax.Precision.HIGHEST)

def solve_with(factor, source):
    inner = jax.scipy.linalg.solve_triangular(factor, source, lower=True)
    return jax.scipy.linalg.solve_triangular(factor, inner, lower=True, trans=1)

def normal_system(model_channel, data_channel, keep_channel, station_one, station_two):
    coherence = model_channel.astype(jnp.float32).T
    weights = keep_channel.astype(jnp.float32)
    row_count = coherence.shape[0]
    outer_terms = (weights[:, None, None] * coherence[:, :, None] * coherence[:, None, :]).reshape(row_count, DIRECTIONS * DIRECTIONS)
    pair_one = station_one * STATIONS + station_two
    pair_two = station_two * STATIONS + station_one
    crossed = jax.ops.segment_sum(outer_terms, pair_one, STATIONS * STATIONS) + jax.ops.segment_sum(outer_terms, pair_two, STATIONS * STATIONS)
    selfed = jax.ops.segment_sum(outer_terms, station_one, STATIONS) + jax.ops.segment_sum(outer_terms, station_two, STATIONS)
    crossed = crossed.reshape(STATIONS, STATIONS, DIRECTIONS, DIRECTIONS)
    identity = jnp.eye(STATIONS, dtype=jnp.float32)
    blocks = crossed + identity[:, :, None, None] * selfed.reshape(STATIONS, 1, DIRECTIONS, DIRECTIONS)
    normal = blocks.transpose(2, 0, 3, 1).reshape(DIRECTIONS * STATIONS, DIRECTIONS * STATIONS)
    projected = (weights * data_channel)[:, None] * coherence
    target = jax.ops.segment_sum(projected, station_one, STATIONS) + jax.ops.segment_sum(projected, station_two, STATIONS)
    return (normal, target.T.reshape(DIRECTIONS * STATIONS))

def reference(model_vis, observed, row_keep, station_one, station_two, smoothness):
    block_width = smoothness.shape[0]
    identity = jnp.eye(block_width, dtype=jnp.float32)
    channels = jnp.arange(CHANNELS, dtype=jnp.int32)

    def forward(carried, channel_items):
        previous_inverse, previous_vector = carried
        model_channel, data_channel, keep_channel, channel = channel_items
        normal, target = normal_system(model_channel, data_channel, keep_channel, station_one, station_two)
        neighbours = 2.0 - (channel == 0).astype(jnp.float32) - (channel == CHANNELS - 1).astype(jnp.float32)
        pivot_block = normal + jnp.diag(ridge_weight + neighbours * smoothness) - smoothness[:, None] * previous_inverse * smoothness[None, :]
        source = target + smoothness * previous_vector
        factor = jnp.linalg.cholesky(pivot_block)
        inverse = solve_with(factor, identity)
        solved = product(inverse, source)
        return ((inverse, solved), (inverse * smoothness[None, :], solved))
    start = (jnp.zeros((block_width, block_width), jnp.float32), jnp.zeros((block_width,), jnp.float32))
    finished, stacked = lax.scan(forward, start, (model_vis, observed, row_keep, channels))

    def backward(later, channel_items):
        coupling, solved = channel_items
        current = solved + product(coupling, later)
        return (current, current)
    finished_back, gains = lax.scan(backward, jnp.zeros((block_width,), jnp.float32), stacked, reverse=True)
    return gains
```

```python
import functools

import jax
import jax.numpy as jnp
from jax import lax
from jax.experimental import pallas as pl
from jax.experimental.pallas import tpu as pltpu
from jax.sharding import PartitionSpec as P

ridge_weight = 1.0
PANEL = 128
SUB = 8
PIVOTS = 4
BLK = 32
HIGHEST = lax.Precision.HIGHEST


def mm(left, right, dims=((1,), (0,))):
    return lax.dot_general(
        left, right, (dims, ((), ())), precision=HIGHEST, preferred_element_type=jnp.float32
    )


NT = ((1,), (1,))
TN = ((0,), (0,))


def factor_panel(block):
    size = block.shape[0]
    strips = size // SUB
    lane = lax.broadcasted_iota(jnp.int32, (SUB, size), 1)
    sub = lax.broadcasted_iota(jnp.int32, (SUB, size), 0)
    index = range(PIVOTS)

    def spread(value):
        return jnp.broadcast_to(value, (SUB, size))

    def columns(value, k):
        return [jnp.take_along_axis(value, jnp.full((SUB, size), k + j, jnp.int32), axis=1) for j in index]

    a = [block[t * SUB : (t + 1) * SUB, :] for t in range(strips)]
    done = [jnp.zeros((SUB, size), jnp.float32) for _ in range(strips)]

    for k in range(0, size, PIVOTS):
        home, offset = k // SUB, k % SUB
        last = (k // BLK + 1) * BLK // SUB
        cols = columns(a[home], k)
        e = [[spread(cols[j][offset + i : offset + i + 1, :]) for j in range(i + 1)] for i in index]
        inverse, low = [], [[None] * PIVOTS for _ in index]
        for m in index:
            inverse.append(1.0 / e[m][m])
            for i in range(m + 1, PIVOTS):
                low[i][m] = e[i][m] * inverse[m]
                for j in range(m + 1, i + 1):
                    e[i][j] = e[i][j] - low[i][m] * e[j][m]
        inside = (lane >= k) & (lane < k + PIVOTS)
        u = []
        for i in index:
            row = spread(a[home][offset + i : offset + i + 1, :])
            value = jnp.where(inside, jnp.where(lane == k + i, 1.0, 0.0), row)
            for m in range(i):
                value = value - low[i][m] * u[m]
            u.append(value)
        s = [u[i] * inverse[i] for i in index]
        for i in reversed(index):
            for m in range(i + 1, PIVOTS):
                s[i] = s[i] - low[m][i] * s[m]
        for t in range((k + PIVOTS) // SUB, last):
            c = cols if t == home else columns(a[t], k)
            value = jnp.where(inside, 0.0, a[t])
            for j in index:
                value = value - c[j] * s[j]
            a[t] = value
        for i in index:
            root = lax.rsqrt(e[i][i])
            root = root * (1.5 - 0.5 * e[i][i] * root * root)
            done[home] = jnp.where(sub == offset + i, root * u[i], done[home])
        if offset + PIVOTS == SUB:
            keep = (lane <= sub + home * SUB) | (lane >= last * SUB)
            done[home] = jnp.where(keep, done[home], 0.0)
        if k + PIVOTS == last * SUB and last < strips:
            first = last - BLK // SUB
            rows = jnp.concatenate(done[first:last], axis=0)
            own = (lane >= first * SUB) & (lane < last * SUB)
            rest = jnp.concatenate([jnp.where(own, 0.0, a[t]) for t in range(last, strips)], axis=0)
            f = jnp.transpose(rows[:, last * SUB:])
            rest = rest - mm(f, rows)
            for t in range(last, strips):
                a[t] = rest[(t - last) * SUB : (t - last + 1) * SUB, :]
            for t in range(first, last):
                done[t] = jnp.where(lane < last * SUB, done[t], 0.0)
    return jnp.concatenate(done, axis=0)

def pairs(width):
    count = width // PANEL
    return [(r, c, r * (r + 1) // 2 + c) for r in range(count) for c in range(r + 1)]


def cut(index):
    return slice(index * PANEL, (index + 1) * PANEL)


def payload_rows(width):
    return len(pairs(width)) * PANEL + width // PANEL * SUB


def put_line(packed_ref, value):
    width = value.shape[1]
    base = len(pairs(width)) * PANEL
    for b in range(width // PANEL):
        packed_ref[base + b * SUB : base + (b + 1) * SUB, :] = value[:, cut(b)]


def get_line(packed_ref, width):
    base = len(pairs(width)) * PANEL
    return jnp.concatenate(
        [packed_ref[base + b * SUB : base + (b + 1) * SUB, :] for b in range(width // PANEL)], axis=1
    )


def fill_square(square_ref, packed_ref):
    for r, c, at in pairs(square_ref.shape[0]):
        piece = packed_ref[cut(at), :]
        square_ref[cut(r), cut(c)] = piece
        if r != c:
            square_ref[cut(c), cut(r)] = jnp.transpose(piece)


def factor(x_ref):
    width = x_ref.shape[0]
    count = width // PANEL

    @pl.loop(0, count)
    def _(step):
        own = pl.ds(pl.multiple_of(step * PANEL, PANEL), PANEL)
        x_ref[own, own] = factor_panel(x_ref[own, own])
        for p in range(count):

            @pl.when(step == p)
            def _():
                lo, hi = p * PANEL, (p + 1) * PANEL
                root = x_ref[lo:hi, lo:hi]
                if p:
                    x_ref[lo:hi, :lo] = mm(root, x_ref[lo:hi, :lo])
                if hi < width:
                    f = mm(x_ref[hi:, lo:hi], root, NT)
                    x_ref[hi:, hi:] = x_ref[hi:, hi:] - mm(f, f, NT)
                    if p:
                        x_ref[hi:, :lo] = x_ref[hi:, :lo] - mm(f, x_ref[lo:hi, :lo])
                    x_ref[hi:, lo:hi] = -mm(f, root)

    for r in range(count - 1):
        x_ref[cut(r), (r + 1) * PANEL :] = jnp.zeros((PANEL, width - (r + 1) * PANEL), jnp.float32)


def first_kernel(diag_ref, source_ref, across_ref, coupling_ref, packed_ref, y_ref, x_ref, t_ref):
    width = diag_ref.shape[0]
    x_ref[...] = diag_ref[...]
    factor(x_ref)
    y = mm(mm(source_ref[...], x_ref[...], NT), x_ref[...])
    y_ref[...] = y
    put_line(packed_ref, y * across_ref[...])
    x_ref[...] = x_ref[...] * across_ref[...]
    for r, c, _ in pairs(width):
        t_ref[cut(c), cut(r)] = jnp.transpose(x_ref[cut(r), cut(c)])
    for r in range(width // PANEL):
        value = mm(t_ref[cut(r), r * PANEL :], x_ref[r * PANEL :, : (r + 1) * PANEL])
        for c in range(r + 1):
            packed_ref[cut(r * (r + 1) // 2 + c), :] = value[:, cut(c)]
    fill_square(coupling_ref, packed_ref)


def level_kernel(first, flag_ref, diag_ref, rise_ref, fall_ref, below_ref, *refs):
    if first:
        source_ref, *outs, above_ref = refs
    else:
        above_ref, source_ref, *outs = refs
    diag_out, source_out, up_ref, down_ref, cross_ref, c_ref, line_ref, x_ref = outs
    width = diag_ref.shape[0]
    for r, c, at in pairs(width):
        diag_out[cut(r), cut(c)] = (
            diag_ref[cut(r), cut(c)] - rise_ref[cut(at), :] - fall_ref[cut(at), :]
        )
    source_out[...] = source_ref[...] + get_line(rise_ref, width) + get_line(fall_ref, width)

    @pl.when(flag_ref[0] == 1)
    def _():
        if first:
            fill_square(above_ref, fall_ref)
        x_ref[...] = diag_out[...]
        factor(x_ref)
        half = width // 2
        for side, ref in enumerate((below_ref, above_ref)):
            c_ref[side, :, :half] = mm(ref[:, :half], x_ref[:half, :half], NT)
            c_ref[side, :, half:] = mm(ref[...], x_ref[half:, :], NT)
        line = mm(source_out[...], x_ref[...], NT)
        line_ref[...] = line
        cross_ref[...] = mm(c_ref[flag_ref[1]], c_ref[1 - flag_ref[1]], NT)
        for side, ref in enumerate((down_ref, up_ref)):
            put_line(ref, mm(line, c_ref[side], NT))
            for r in range(width // PANEL):
                value = mm(c_ref[side, cut(r), :], c_ref[side, : (r + 1) * PANEL, :], NT)
                for c in range(r + 1):
                    ref[cut(r * (r + 1) // 2 + c), :] = value[:, cut(c)]


def last_kernel(diag_ref, rise_ref, source_ref, y_ref, x_ref):
    width = diag_ref.shape[0]
    for r, c, at in pairs(width):
        x_ref[cut(r), cut(c)] = diag_ref[cut(r), cut(c)] - rise_ref[cut(at), :]
    factor(x_ref)
    source = source_ref[...] + get_line(rise_ref, width)
    y_ref[...] = mm(mm(source, x_ref[...], NT), x_ref[...])


def back_kernel(flag_ref, below_ref, above_ref, gains_ref, c_ref, line_ref, x_ref, out_ref):
    out_ref[...] = gains_ref[...]

    @pl.when(flag_ref[0] == 1)
    def _():
        line = line_ref[...] + mm(below_ref[...], c_ref[0]) + mm(above_ref[...], c_ref[1])
        out_ref[...] = mm(line, x_ref[...])


def call(kernel, outs, *operands, scratch=()):
    vmem = pl.BlockSpec(memory_space=pltpu.VMEM)
    smem = pl.BlockSpec(memory_space=pltpu.SMEM)
    return pl.pallas_call(
        kernel,
        out_shape=[jax.ShapeDtypeStruct(o, jnp.float32) for o in outs],
        in_specs=[smem if o.dtype == jnp.int32 else vmem for o in operands],
        out_specs=[vmem] * len(outs),
        scratch_shapes=[pltpu.VMEM(s, jnp.float32) for s in scratch],
        compiler_params=pltpu.CompilerParams(vmem_limit_bytes=48 << 20),
    )(*operands)

def normal_kernel(vis_ref, obs_ref, keep_ref, one_ref, two_ref, normal_ref, target_ref):
    padded = normal_ref.shape[1]
    directions, rows = vis_ref.shape[1], vis_ref.shape[2]
    stations = padded // directions

    @pl.when(pl.program_id(1) == 0)
    def _():
        normal_ref[...] = jnp.zeros_like(normal_ref)
        target_ref[...] = jnp.zeros_like(target_ref)

    station = lax.broadcasted_iota(jnp.int32, (stations, rows), 0)
    touched = (station == one_ref[...]) | (station == two_ref[...])
    keep = keep_ref[0].astype(jnp.float32)
    vis = vis_ref[0].astype(jnp.float32)
    kept = touched & (keep > 0.0)
    plain = jnp.concatenate(
        [jnp.where(touched, vis[d : d + 1, :], 0.0) for d in range(directions)], axis=0
    ).astype(jnp.bfloat16)
    weighted = jnp.concatenate(
        [jnp.where(kept, vis[d : d + 1, :], 0.0) for d in range(directions)], axis=0
    ).astype(jnp.bfloat16)
    normal_ref[0] += lax.dot_general(
        weighted, plain, (NT, ((), ())), preferred_element_type=jnp.float32
    )
    data = obs_ref[0]
    high = data.astype(jnp.bfloat16).astype(jnp.float32)
    middle = (data - high).astype(jnp.bfloat16).astype(jnp.float32)
    low = data - high - middle
    pieces = jnp.concatenate([high, middle, low, jnp.zeros((5, rows), jnp.float32)], axis=0)
    target_ref[0] += lax.dot_general(
        pieces.astype(jnp.bfloat16), weighted, (NT, ((), ())), preferred_element_type=jnp.float32
    )


def normals(model_vis, observed, row_keep, station_one, station_two, padded):
    channels, directions, rows = model_vis.shape
    chunk = 1024 if rows % 1024 == 0 else rows
    return pl.pallas_call(
        normal_kernel,
        grid=(channels, rows // chunk),
        out_shape=[
            jax.ShapeDtypeStruct((channels, padded, padded), jnp.float32),
            jax.ShapeDtypeStruct((channels, 8, padded), jnp.float32),
        ],
        in_specs=[
            pl.BlockSpec((1, directions, chunk), lambda f, r: (f, 0, r)),
            pl.BlockSpec((1, 1, chunk), lambda f, r: (f, 0, r)),
            pl.BlockSpec((1, 1, chunk), lambda f, r: (f, 0, r)),
            pl.BlockSpec((1, chunk), lambda f, r: (0, r)),
            pl.BlockSpec((1, chunk), lambda f, r: (0, r)),
        ],
        out_specs=[
            pl.BlockSpec((1, padded, padded), lambda f, r: (f, 0, 0)),
            pl.BlockSpec((1, 8, padded), lambda f, r: (f, 0, 0)),
        ],
        compiler_params=pltpu.CompilerParams(vmem_limit_bytes=48 << 20),
    )(
        model_vis,
        observed.reshape(channels, 1, rows),
        row_keep.reshape(channels, 1, rows),
        station_one.reshape(1, rows),
        station_two.reshape(1, rows),
    )


def move(block, route):
    return lax.ppermute(block, "freq", route)


def body(model_vis, observed, row_keep, station_one, station_two, smoothness):
    channels, directions, _ = model_vis.shape
    assert channels == 2
    devices = lax.axis_size("freq")
    assert devices & (devices - 1) == 0
    position = lax.axis_index("freq")
    stations = smoothness.shape[0] // directions
    slots = -(-stations // 64) * 64
    width = directions * slots
    square, line = (width, width), (SUB, width)
    packed = (payload_rows(width), PANEL)
    smooth = jnp.pad(
        smoothness.reshape(directions, stations), ((0, 0), (0, slots - stations))
    ).reshape(width)

    normal, pieces = normals(model_vis, observed, row_keep, station_one, station_two, width)
    targets = jnp.sum(pieces, axis=1)
    identity = jnp.eye(width, dtype=jnp.float32)

    def diagonal(local):
        channel = position * channels + local
        neighbours = (
            2.0
            - (channel == 0).astype(jnp.float32)
            - (channel == channels * devices - 1).astype(jnp.float32)
        )
        return normal[local] + identity * (ridge_weight + neighbours * smooth)[:, None]

    def as_line(vector):
        return jnp.pad(vector[None, :], ((0, SUB - 1), (0, 0)))

    coupling, rise, y0 = call(
        first_kernel, (square, packed, line),
        diagonal(0), as_line(targets[0]), smooth[None, :], scratch=(square, square),
    )
    fall = move(rise, [(i, i - 1) for i in range(1, devices)])
    diag, source, below, above = diagonal(1), as_line(targets[1]), coupling, None

    levels = (devices - 1).bit_length()
    kept = []
    for level in range(levels):
        stride = 1 << level
        phase = lax.rem(position + 1, 4 * stride)
        mine = lax.rem(phase, 2 * stride) == stride
        drop = (phase == 3 * stride).astype(jnp.int32)
        flag = jnp.stack([mine.astype(jnp.int32), drop])
        sides = (below,) if level == 0 else (below, above)
        diag, source, up, down, cross, c, solved, inverse = call(
            functools.partial(level_kernel, level == 0),
            (square, line, packed, packed, square, (2,) + square, line, square),
            flag, diag, rise, fall, *sides, source, scratch=(square,) * (level == 0),
        )
        kept.append((flag, c, solved, inverse))
        gone = range(stride - 1, devices, 2 * stride)
        rises = [(i, i + stride) for i in gone]
        falls = [(i, i - stride) for i in gone if i >= stride]
        next_gone = range(2 * stride - 1, devices, 4 * stride) if level + 1 < levels else ()
        if next_gone:
            below = move(cross, [(i, j) for i, j in rises if j in next_gone])
            above = move(cross, [(i, j) for i, j in falls if j in next_gone])
        rise = move(up, rises)
        if falls:
            fall = move(down, falls)
    (gains,) = call(last_kernel, (line,), diag, rise, source, scratch=(square,))
    for level in reversed(range(levels)):
        stride = 1 << level
        flag, c, solved, inverse = kept[level]
        gone = range(stride - 1, devices, 2 * stride)
        from_above = move(gains, [(i + stride, i) for i in gone])
        falling = [(i - stride, i) for i in gone if i >= stride]
        from_below = move(gains, falling) if falling else jnp.zeros_like(gains)
        (gains,) = call(back_kernel, (line,), flag, from_below, from_above, gains, c, solved, inverse)
    earlier = move(gains, [(i, i + 1) for i in range(devices - 1)])
    scale = jnp.where(smooth > 0, 1.0 / jnp.where(smooth > 0, smooth, 1.0), 0.0)
    first = y0 + mm(earlier + gains, coupling) * scale[None, :]
    both = jnp.stack([first[0], gains[0]])
    return both.reshape(channels, directions, slots)[:, :, :stations].reshape(
        channels, directions * stations
    )


def solution(mesh):
    placed = (P("freq", None, None), P("freq", None), P("freq", None), P(), P(), P())
    return jax.shard_map(
        body, mesh=mesh, in_specs=placed, out_specs=P("freq", None), check_vma=False
    )
```

```python
import functools

import jax
import jax.numpy as jnp
from jax import lax
from jax.experimental import pallas as pl
from jax.experimental.pallas import tpu as pltpu
from jax.sharding import PartitionSpec as P

ridge_weight = 1.0
PANEL = 128
SUB = 8
PIVOTS = 8
BLK = 32
VMEM_LIMIT = 28 << 20
HIGHEST = lax.Precision.HIGHEST


def mm(left, right, dims=((1,), (0,))):
    return lax.dot_general(
        left, right, (dims, ((), ())), precision=HIGHEST, preferred_element_type=jnp.float32
    )


NT = ((1,), (1,))
TN = ((0,), (0,))


def factor_panel(block):
    size = block.shape[0]
    strips = size // SUB
    lane = lax.broadcasted_iota(jnp.int32, (SUB, size), 1)
    sub = lax.broadcasted_iota(jnp.int32, (SUB, size), 0)
    index = range(PIVOTS)

    def spread(value):
        return jnp.broadcast_to(value, (SUB, size))

    def columns(value, k):
        return [jnp.take_along_axis(value, jnp.full((SUB, size), k + j, jnp.int32), axis=1) for j in index]

    a = [block[t * SUB : (t + 1) * SUB, :] for t in range(strips)]
    done = [jnp.zeros((SUB, size), jnp.float32) for _ in range(strips)]

    for k in range(0, size, PIVOTS):
        home, offset = k // SUB, k % SUB
        last = (k // BLK + 1) * BLK // SUB
        cols = columns(a[home], k)
        e = [[spread(cols[j][offset + i : offset + i + 1, :]) for j in range(i + 1)] for i in index]
        inverse, low = [], [[None] * PIVOTS for _ in index]
        for m in index:
            inverse.append(1.0 / e[m][m])
            for i in range(m + 1, PIVOTS):
                low[i][m] = e[i][m] * inverse[m]
                for j in range(m + 1, i + 1):
                    e[i][j] = e[i][j] - low[i][m] * e[j][m]
        inside = (lane >= k) & (lane < k + PIVOTS)
        u = []
        for i in index:
            row = spread(a[home][offset + i : offset + i + 1, :])
            value = jnp.where(inside, jnp.where(lane == k + i, 1.0, 0.0), row)
            for m in range(i):
                value = value - low[i][m] * u[m]
            u.append(value)
        s = [u[i] * inverse[i] for i in index]
        for i in reversed(index):
            for m in range(i + 1, PIVOTS):
                s[i] = s[i] - low[m][i] * s[m]
        for t in range((k + PIVOTS) // SUB, last):
            c = cols if t == home else columns(a[t], k)
            value = jnp.where(inside, 0.0, a[t])
            for j in index:
                value = value - c[j] * s[j]
            a[t] = value
        for i in index:
            root = lax.rsqrt(e[i][i])
            root = root * (1.5 - 0.5 * e[i][i] * root * root)
            done[home] = jnp.where(sub == offset + i, root * u[i], done[home])
        if offset + PIVOTS == SUB:
            keep = (lane <= sub + home * SUB) | (lane >= last * SUB)
            done[home] = jnp.where(keep, done[home], 0.0)
        if k + PIVOTS == last * SUB and last < strips:
            first = last - BLK // SUB
            rows = jnp.concatenate(done[first:last], axis=0)
            own = (lane >= first * SUB) & (lane < last * SUB)
            rest = jnp.concatenate([jnp.where(own, 0.0, a[t]) for t in range(last, strips)], axis=0)
            f = jnp.transpose(rows[:, last * SUB:])
            rest = rest - mm(f, rows)
            for t in range(last, strips):
                a[t] = rest[(t - last) * SUB : (t - last + 1) * SUB, :]
            for t in range(first, last):
                done[t] = jnp.where(lane < last * SUB, done[t], 0.0)
    return jnp.concatenate(done, axis=0)

def pairs(width):
    count = width // PANEL
    return [(r, c, r * (r + 1) // 2 + c) for r in range(count) for c in range(r + 1)]


def cut(index):
    return slice(index * PANEL, (index + 1) * PANEL)


def payload_rows(width):
    return len(pairs(width)) * PANEL + width // PANEL * SUB


def put_line(packed_ref, value):
    width = value.shape[1]
    base = len(pairs(width)) * PANEL
    for b in range(width // PANEL):
        packed_ref[base + b * SUB : base + (b + 1) * SUB, :] = value[:, cut(b)]


def get_line(packed_ref, width):
    base = len(pairs(width)) * PANEL
    return jnp.concatenate(
        [packed_ref[base + b * SUB : base + (b + 1) * SUB, :] for b in range(width // PANEL)], axis=1
    )


def fill_square(square_ref, packed_ref):
    for r, c, at in pairs(square_ref.shape[0]):
        piece = packed_ref[cut(at), :]
        square_ref[cut(r), cut(c)] = piece
        if r != c:
            square_ref[cut(c), cut(r)] = jnp.transpose(piece)


def factor(x_ref):
    width = x_ref.shape[0]
    count = width // PANEL

    @pl.loop(0, count)
    def _(step):
        own = pl.ds(pl.multiple_of(step * PANEL, PANEL), PANEL)
        x_ref[own, own] = factor_panel(x_ref[own, own])
        for p in range(count):

            @pl.when(step == p)
            def _():
                lo, hi = p * PANEL, (p + 1) * PANEL
                root = x_ref[lo:hi, lo:hi]
                if p:
                    x_ref[lo:hi, :lo] = mm(root, x_ref[lo:hi, :lo])
                if hi < width:
                    f = mm(x_ref[hi:, lo:hi], root, NT)
                    x_ref[hi:, hi:] = x_ref[hi:, hi:] - mm(f, f, NT)
                    if p:
                        x_ref[hi:, :lo] = x_ref[hi:, :lo] - mm(f, x_ref[lo:hi, :lo])
                    x_ref[hi:, lo:hi] = -mm(f, root)

    for r in range(count - 1):
        x_ref[cut(r), (r + 1) * PANEL :] = jnp.zeros((PANEL, width - (r + 1) * PANEL), jnp.float32)


def first_kernel(
    diag_ref, source_ref, across_ref, coupling_ref, packed_ref, y_ref, c_ref, line_ref, x_ref, t_ref
):
    width = diag_ref.shape[0]
    x_ref[...] = diag_ref[...]
    factor(x_ref)
    y = mm(mm(source_ref[...], x_ref[...], NT), x_ref[...])
    y_ref[...] = y
    put_line(packed_ref, y * across_ref[...])
    x_ref[...] = x_ref[...] * across_ref[...]
    for r, c, _ in pairs(width):
        t_ref[cut(c), cut(r)] = jnp.transpose(x_ref[cut(r), cut(c)])
    for r in range(width // PANEL):
        value = mm(t_ref[cut(r), r * PANEL :], x_ref[r * PANEL :, : (r + 1) * PANEL])
        for c in range(r + 1):
            packed_ref[cut(r * (r + 1) // 2 + c), :] = value[:, cut(c)]
    fill_square(coupling_ref, packed_ref)


def level_kernel(first, flag_ref, diag_ref, rise_ref, fall_ref, below_ref, *refs):
    if first:
        source_ref, _, _, _, *outs, above_ref = refs
    else:
        above_ref, source_ref, _, _, _, *outs = refs
    diag_out, source_out, up_ref, down_ref, cross_ref, c_ref, line_ref, x_ref = outs
    width = diag_ref.shape[0]
    for r, c, at in pairs(width):
        diag_out[cut(r), cut(c)] = (
            diag_ref[cut(r), cut(c)] - rise_ref[cut(at), :] - fall_ref[cut(at), :]
        )
    source_out[...] = source_ref[...] + get_line(rise_ref, width) + get_line(fall_ref, width)

    @pl.when(flag_ref[0] == 1)
    def _():
        if first:
            fill_square(above_ref, fall_ref)
        x_ref[...] = diag_out[...]
        factor(x_ref)
        half = width // 2
        for side, ref in enumerate((below_ref, above_ref)):
            c_ref[side, :, :half] = mm(ref[:, :half], x_ref[:half, :half], NT)
            c_ref[side, :, half:] = mm(ref[...], x_ref[half:, :], NT)
        line = mm(source_out[...], x_ref[...], NT)
        line_ref[...] = line
        cross_ref[...] = mm(c_ref[flag_ref[1]], c_ref[1 - flag_ref[1]], NT)
        for side, ref in enumerate((down_ref, up_ref)):
            put_line(ref, mm(line, c_ref[side], NT))
            for r in range(width // PANEL):
                value = mm(c_ref[side, cut(r), :], c_ref[side, : (r + 1) * PANEL, :], NT)
                for c in range(r + 1):
                    ref[cut(r * (r + 1) // 2 + c), :] = value[:, cut(c)]


def last_kernel(diag_ref, rise_ref, source_ref, y_ref, x_ref):
    width = diag_ref.shape[0]
    for r, c, at in pairs(width):
        x_ref[cut(r), cut(c)] = diag_ref[cut(r), cut(c)] - rise_ref[cut(at), :]
    factor(x_ref)
    source = source_ref[...] + get_line(rise_ref, width)
    y_ref[...] = mm(mm(source, x_ref[...], NT), x_ref[...])


def back_kernel(flag_ref, below_ref, above_ref, gains_ref, c_ref, line_ref, x_ref, out_ref):
    out_ref[...] = gains_ref[...]

    @pl.when(flag_ref[0] == 1)
    def _():
        line = line_ref[...] + mm(below_ref[...], c_ref[0]) + mm(above_ref[...], c_ref[1])
        out_ref[...] = mm(line, x_ref[...])


def call(kernel, outs, *operands, scratch=(), aliases=None):
    vmem = pl.BlockSpec(memory_space=pltpu.VMEM)
    smem = pl.BlockSpec(memory_space=pltpu.SMEM)
    return pl.pallas_call(
        kernel,
        out_shape=[jax.ShapeDtypeStruct(o, jnp.float32) for o in outs],
        in_specs=[smem if o.dtype == jnp.int32 else vmem for o in operands],
        out_specs=[vmem] * len(outs),
        scratch_shapes=[pltpu.VMEM(s, jnp.float32) for s in scratch],
        input_output_aliases=aliases or {},
        compiler_params=pltpu.CompilerParams(vmem_limit_bytes=VMEM_LIMIT),
    )(*operands)

def normal_kernel(vis_ref, obs_ref, keep_ref, one_ref, two_ref, normal_ref, target_ref):
    padded = normal_ref.shape[1]
    directions, rows = vis_ref.shape[1], vis_ref.shape[2]
    stations = padded // directions

    @pl.when(pl.program_id(1) == 0)
    def _():
        normal_ref[...] = jnp.zeros_like(normal_ref)
        target_ref[...] = jnp.zeros_like(target_ref)

    station = lax.broadcasted_iota(jnp.int32, (stations, rows), 0)
    touched = (station == one_ref[...]) | (station == two_ref[...])
    keep = keep_ref[0].astype(jnp.float32)
    vis = vis_ref[0].astype(jnp.float32)
    kept = touched & (keep > 0.0)
    plain = jnp.concatenate(
        [jnp.where(touched, vis[d : d + 1, :], 0.0) for d in range(directions)], axis=0
    ).astype(jnp.bfloat16)
    weighted = jnp.concatenate(
        [jnp.where(kept, vis[d : d + 1, :], 0.0) for d in range(directions)], axis=0
    ).astype(jnp.bfloat16)
    normal_ref[0] += lax.dot_general(
        weighted, plain, (NT, ((), ())), preferred_element_type=jnp.float32
    )
    data = obs_ref[0]
    high = data.astype(jnp.bfloat16).astype(jnp.float32)
    middle = (data - high).astype(jnp.bfloat16).astype(jnp.float32)
    low = data - high - middle
    pieces = jnp.concatenate([high, middle, low, jnp.zeros((5, rows), jnp.float32)], axis=0)
    target_ref[0] += lax.dot_general(
        pieces.astype(jnp.bfloat16), weighted, (NT, ((), ())), preferred_element_type=jnp.float32
    )


def normals(model_vis, observed, row_keep, station_one, station_two, padded):
    channels, directions, rows = model_vis.shape
    chunk = 1024 if rows % 1024 == 0 else rows
    return pl.pallas_call(
        normal_kernel,
        grid=(channels, rows // chunk),
        out_shape=[
            jax.ShapeDtypeStruct((channels, padded, padded), jnp.float32),
            jax.ShapeDtypeStruct((channels, 8, padded), jnp.float32),
        ],
        in_specs=[
            pl.BlockSpec((1, directions, chunk), lambda f, r: (f, 0, r)),
            pl.BlockSpec((1, 1, chunk), lambda f, r: (f, 0, r)),
            pl.BlockSpec((1, 1, chunk), lambda f, r: (f, 0, r)),
            pl.BlockSpec((1, chunk), lambda f, r: (0, r)),
            pl.BlockSpec((1, chunk), lambda f, r: (0, r)),
        ],
        out_specs=[
            pl.BlockSpec((1, padded, padded), lambda f, r: (f, 0, 0)),
            pl.BlockSpec((1, 8, padded), lambda f, r: (f, 0, 0)),
        ],
        compiler_params=pltpu.CompilerParams(vmem_limit_bytes=48 << 20),
    )(
        model_vis,
        observed.reshape(channels, 1, rows),
        row_keep.reshape(channels, 1, rows),
        station_one.reshape(1, rows),
        station_two.reshape(1, rows),
    )


def move(block, route):
    return lax.ppermute(block, "freq", route)


def body(model_vis, observed, row_keep, station_one, station_two, smoothness):
    channels, directions, _ = model_vis.shape
    assert channels == 2
    devices = lax.axis_size("freq")
    assert devices & (devices - 1) == 0
    position = lax.axis_index("freq")
    stations = smoothness.shape[0] // directions
    slots = -(-stations // 64) * 64
    width = directions * slots
    square, line = (width, width), (SUB, width)
    packed = (payload_rows(width), PANEL)
    smooth = jnp.pad(
        smoothness.reshape(directions, stations), ((0, 0), (0, slots - stations))
    ).reshape(width)

    normal, pieces = normals(model_vis, observed, row_keep, station_one, station_two, width)
    targets = jnp.sum(pieces, axis=1)
    identity = jnp.eye(width, dtype=jnp.float32)

    def diagonal(local):
        channel = position * channels + local
        neighbours = (
            2.0
            - (channel == 0).astype(jnp.float32)
            - (channel == channels * devices - 1).astype(jnp.float32)
        )
        return normal[local] + identity * (ridge_weight + neighbours * smooth)[:, None]

    def as_line(vector):
        return jnp.pad(vector[None, :], ((0, SUB - 1), (0, 0)))

    coupling, rise, y0, c, solved, inverse = call(
        first_kernel, (square, packed, line, (2,) + square, line, square),
        diagonal(0), as_line(targets[0]), smooth[None, :], scratch=(square,),
    )
    fall = move(rise, [(i, i - 1) for i in range(1, devices)])
    diag, source, below, above = diagonal(1), as_line(targets[1]), coupling, None

    levels = (devices - 1).bit_length()
    kept = []
    for level in range(levels):
        stride = 1 << level
        phase = lax.rem(position + 1, 4 * stride)
        mine = lax.rem(phase, 2 * stride) == stride
        drop = (phase == 3 * stride).astype(jnp.int32)
        flag = jnp.stack([mine.astype(jnp.int32), drop])
        sides = (below,) if level == 0 else (below, above)
        diag, source, up, down, cross, c, solved, inverse = call(
            functools.partial(level_kernel, level == 0),
            (square, line, packed, packed, square, (2,) + square, line, square),
            flag, diag, rise, fall, *sides, source, c, solved, inverse,
            scratch=(square,) * (level == 0),
            aliases={1: 0, len(sides) + 4: 1, len(sides) + 5: 5, len(sides) + 6: 6, len(sides) + 7: 7},
        )
        kept.append(flag)
        gone = range(stride - 1, devices, 2 * stride)
        rises = [(i, i + stride) for i in gone]
        falls = [(i, i - stride) for i in gone if i >= stride]
        next_gone = range(2 * stride - 1, devices, 4 * stride) if level + 1 < levels else ()
        if next_gone:
            below = move(cross, [(i, j) for i, j in rises if j in next_gone])
            above = move(cross, [(i, j) for i, j in falls if j in next_gone])
        rise = move(up, rises)
        if falls:
            fall = move(down, falls)
    (gains,) = call(last_kernel, (line,), diag, rise, source, scratch=(square,))
    for level in reversed(range(levels)):
        stride = 1 << level
        flag = kept[level]
        gone = range(stride - 1, devices, 2 * stride)
        from_above = move(gains, [(i + stride, i) for i in gone])
        falling = [(i - stride, i) for i in gone if i >= stride]
        from_below = move(gains, falling) if falling else jnp.zeros_like(gains)
        (gains,) = call(back_kernel, (line,), flag, from_below, from_above, gains, c, solved, inverse)
    earlier = move(gains, [(i, i + 1) for i in range(devices - 1)])
    scale = jnp.where(smooth > 0, 1.0 / jnp.where(smooth > 0, smooth, 1.0), 0.0)
    first = y0 + mm(earlier + gains, coupling) * scale[None, :]
    both = jnp.stack([first[0], gains[0]])
    return both.reshape(channels, directions, slots)[:, :, :stations].reshape(
        channels, directions * stations
    )


def solution(mesh):
    placed = (P("freq", None, None), P("freq", None), P("freq", None), P(), P(), P())
    return jax.shard_map(
        body, mesh=mesh, in_specs=placed, out_specs=P("freq", None), check_vma=False
    )
```

```python
import functools

import jax
import jax.numpy as jnp
from jax import lax
from jax.experimental import pallas as pl
from jax.experimental.pallas import tpu as pltpu
from jax.sharding import PartitionSpec as P

ridge_weight = 1.0
PANEL = 128
SUB = 8
PIVOTS = 8
BLK = 32
VMEM_LIMIT = 24 << 20
HIGHEST = lax.Precision.HIGHEST


def mm(left, right, dims=((1,), (0,))):
    return lax.dot_general(
        left, right, (dims, ((), ())), precision=HIGHEST, preferred_element_type=jnp.float32
    )


NT = ((1,), (1,))
TN = ((0,), (0,))


def factor_panel(block):
    size = block.shape[0]
    strips = size // SUB
    lane = lax.broadcasted_iota(jnp.int32, (SUB, size), 1)
    sub = lax.broadcasted_iota(jnp.int32, (SUB, size), 0)
    index = range(PIVOTS)

    def spread(value):
        return jnp.broadcast_to(value, (SUB, size))

    def columns(value, k):
        return [jnp.take_along_axis(value, jnp.full((SUB, size), k + j, jnp.int32), axis=1) for j in index]

    a = [block[t * SUB : (t + 1) * SUB, :] for t in range(strips)]
    done = [jnp.zeros((SUB, size), jnp.float32) for _ in range(strips)]

    for k in range(0, size, PIVOTS):
        home, offset = k // SUB, k % SUB
        last = (k // BLK + 1) * BLK // SUB
        cols = columns(a[home], k)
        e = [[spread(cols[j][offset + i : offset + i + 1, :]) for j in range(i + 1)] for i in index]
        inverse, low = [], [[None] * PIVOTS for _ in index]
        for m in index:
            inverse.append(1.0 / e[m][m])
            for i in range(m + 1, PIVOTS):
                low[i][m] = e[i][m] * inverse[m]
                for j in range(m + 1, i + 1):
                    e[i][j] = e[i][j] - low[i][m] * e[j][m]
        inside = (lane >= k) & (lane < k + PIVOTS)
        u = []
        for i in index:
            row = spread(a[home][offset + i : offset + i + 1, :])
            value = jnp.where(inside, jnp.where(lane == k + i, 1.0, 0.0), row)
            for m in range(i):
                value = value - low[i][m] * u[m]
            u.append(value)
        s = [u[i] * inverse[i] for i in index]
        for i in reversed(index):
            for m in range(i + 1, PIVOTS):
                s[i] = s[i] - low[m][i] * s[m]
        for t in range((k + PIVOTS) // SUB, last):
            c = cols if t == home else columns(a[t], k)
            value = jnp.where(inside, 0.0, a[t])
            for j in index:
                value = value - c[j] * s[j]
            a[t] = value
        for i in index:
            root = lax.rsqrt(e[i][i])
            root = root * (1.5 - 0.5 * e[i][i] * root * root)
            done[home] = jnp.where(sub == offset + i, root * u[i], done[home])
        if offset + PIVOTS == SUB:
            keep = (lane <= sub + home * SUB) | (lane >= last * SUB)
            done[home] = jnp.where(keep, done[home], 0.0)
        if k + PIVOTS == last * SUB and last < strips:
            first = last - BLK // SUB
            rows = jnp.concatenate(done[first:last], axis=0)
            own = (lane >= first * SUB) & (lane < last * SUB)
            rest = jnp.concatenate([jnp.where(own, 0.0, a[t]) for t in range(last, strips)], axis=0)
            f = jnp.transpose(rows[:, last * SUB:])
            rest = rest - mm(f, rows)
            for t in range(last, strips):
                a[t] = rest[(t - last) * SUB : (t - last + 1) * SUB, :]
            for t in range(first, last):
                done[t] = jnp.where(lane < last * SUB, done[t], 0.0)
    return jnp.concatenate(done, axis=0)

def pairs(width):
    count = width // PANEL
    return [(r, c, r * (r + 1) // 2 + c) for r in range(count) for c in range(r + 1)]


def cut(index):
    return slice(index * PANEL, (index + 1) * PANEL)


def payload_rows(width):
    return len(pairs(width)) * PANEL + width // PANEL * SUB


def put_line(packed_ref, value):
    width = value.shape[1]
    base = len(pairs(width)) * PANEL
    for b in range(width // PANEL):
        packed_ref[base + b * SUB : base + (b + 1) * SUB, :] = value[:, cut(b)]


def get_line(packed_ref, width):
    base = len(pairs(width)) * PANEL
    return jnp.concatenate(
        [packed_ref[base + b * SUB : base + (b + 1) * SUB, :] for b in range(width // PANEL)], axis=1
    )


def fill_square(square_ref, packed_ref):
    for r, c, at in pairs(square_ref.shape[0]):
        piece = packed_ref[cut(at), :]
        square_ref[cut(r), cut(c)] = piece
        if r != c:
            square_ref[cut(c), cut(r)] = jnp.transpose(piece)


def factor(x_ref):
    width = x_ref.shape[0]
    count = width // PANEL

    @pl.loop(0, count)
    def _(step):
        own = pl.ds(pl.multiple_of(step * PANEL, PANEL), PANEL)
        x_ref[own, own] = factor_panel(x_ref[own, own])
        for p in range(count):

            @pl.when(step == p)
            def _():
                lo, hi = p * PANEL, (p + 1) * PANEL
                root = x_ref[lo:hi, lo:hi]
                if p:
                    x_ref[lo:hi, :lo] = mm(root, x_ref[lo:hi, :lo])
                if hi < width:
                    f = mm(x_ref[hi:, lo:hi], root, NT)
                    x_ref[hi:, hi:] = x_ref[hi:, hi:] - mm(f, f, NT)
                    if p:
                        x_ref[hi:, :lo] = x_ref[hi:, :lo] - mm(f, x_ref[lo:hi, :lo])
                    x_ref[hi:, lo:hi] = -mm(f, root)

    for r in range(count - 1):
        x_ref[cut(r), (r + 1) * PANEL :] = jnp.zeros((PANEL, width - (r + 1) * PANEL), jnp.float32)


def first_kernel(
    diag_ref, source_ref, across_ref, coupling_ref, packed_ref, y_ref, c_ref, line_ref, x_ref, t_ref
):
    width = diag_ref.shape[0]
    x_ref[...] = diag_ref[...]
    factor(x_ref)
    y = mm(mm(source_ref[...], x_ref[...], NT), x_ref[...])
    y_ref[...] = y
    put_line(packed_ref, y * across_ref[...])
    x_ref[...] = x_ref[...] * across_ref[...]
    for r, c, _ in pairs(width):
        t_ref[cut(c), cut(r)] = jnp.transpose(x_ref[cut(r), cut(c)])
    for r in range(width // PANEL):
        value = mm(t_ref[cut(r), r * PANEL :], x_ref[r * PANEL :, : (r + 1) * PANEL])
        for c in range(r + 1):
            packed_ref[cut(r * (r + 1) // 2 + c), :] = value[:, cut(c)]
    fill_square(coupling_ref, packed_ref)


def level_kernel(first, flag_ref, diag_ref, rise_ref, fall_ref, below_ref, *refs):
    if first:
        source_ref, _, _, _, *outs = refs
    else:
        above_ref, source_ref, _, _, _, *outs = refs
    diag_out, source_out, up_out, down_out, cross_out, c_ref, line_ref, x_ref, *holds = outs
    below_hold, above_hold, up_ref, down_ref, cross_ref, sems = holds
    width = diag_ref.shape[0]
    for r, c, at in pairs(width):
        diag_out[cut(r), cut(c)] = (
            diag_ref[cut(r), cut(c)] - rise_ref[cut(at), :] - fall_ref[cut(at), :]
        )
    source_out[...] = source_ref[...] + get_line(rise_ref, width) + get_line(fall_ref, width)

    @pl.when(flag_ref[0] == 1)
    def _():
        loads = [pltpu.make_async_copy(below_ref, below_hold, sems.at[0])]
        if first:
            fill_square(above_hold, fall_ref)
        else:
            loads.append(pltpu.make_async_copy(above_ref, above_hold, sems.at[1]))
        for load in loads:
            load.start()
        x_ref[...] = diag_out[...]
        factor(x_ref)
        for load in loads:
            load.wait()
        half = width // 2
        for side, ref in enumerate((below_hold, above_hold)):
            c_ref[side, :, :half] = mm(ref[:, :half], x_ref[:half, :half], NT)
            c_ref[side, :, half:] = mm(ref[...], x_ref[half:, :], NT)
        line = mm(source_out[...], x_ref[...], NT)
        line_ref[...] = line
        cross_ref[...] = mm(c_ref[flag_ref[1]], c_ref[1 - flag_ref[1]], NT)
        stores = [
            pltpu.make_async_copy(ref, out, sems.at[2 + i])
            for i, (ref, out) in enumerate(
                ((cross_ref, cross_out), (down_ref, down_out), (up_ref, up_out))
            )
        ]
        stores[0].start()
        for side, ref in enumerate((down_ref, up_ref)):
            put_line(ref, mm(line, c_ref[side], NT))
            for r in range(width // PANEL):
                value = mm(c_ref[side, cut(r), :], c_ref[side, : (r + 1) * PANEL, :], NT)
                for c in range(r + 1):
                    ref[cut(r * (r + 1) // 2 + c), :] = value[:, cut(c)]
            stores[1 + side].start()
        for store in stores:
            store.wait()


def last_kernel(diag_ref, rise_ref, source_ref, y_ref, x_ref):
    width = diag_ref.shape[0]
    for r, c, at in pairs(width):
        x_ref[cut(r), cut(c)] = diag_ref[cut(r), cut(c)] - rise_ref[cut(at), :]
    factor(x_ref)
    source = source_ref[...] + get_line(rise_ref, width)
    y_ref[...] = mm(mm(source, x_ref[...], NT), x_ref[...])


def back_kernel(flag_ref, below_ref, above_ref, gains_ref, c_ref, line_ref, x_ref, out_ref):
    out_ref[...] = gains_ref[...]

    @pl.when(flag_ref[0] == 1)
    def _():
        line = line_ref[...] + mm(below_ref[...], c_ref[0]) + mm(above_ref[...], c_ref[1])
        out_ref[...] = mm(line, x_ref[...])


def call(kernel, outs, *operands, scratch=(), aliases=None, far_in=(), far_out=(), sems=()):
    vmem = pl.BlockSpec(memory_space=pltpu.VMEM)
    smem = pl.BlockSpec(memory_space=pltpu.SMEM)
    far = pl.BlockSpec(memory_space=pl.ANY)
    return pl.pallas_call(
        kernel,
        out_shape=[jax.ShapeDtypeStruct(o, jnp.float32) for o in outs],
        in_specs=[
            smem if o.dtype == jnp.int32 else far if i in far_in else vmem
            for i, o in enumerate(operands)
        ],
        out_specs=[far if i in far_out else vmem for i in range(len(outs))],
        scratch_shapes=[pltpu.VMEM(s, jnp.float32) for s in scratch] + list(sems),
        input_output_aliases=aliases or {},
        compiler_params=pltpu.CompilerParams(vmem_limit_bytes=VMEM_LIMIT),
    )(*operands)

def normal_kernel(vis_ref, obs_ref, keep_ref, one_ref, two_ref, normal_ref, target_ref):
    padded = normal_ref.shape[1]
    directions, rows = vis_ref.shape[1], vis_ref.shape[2]
    stations = padded // directions

    @pl.when(pl.program_id(1) == 0)
    def _():
        normal_ref[...] = jnp.zeros_like(normal_ref)
        target_ref[...] = jnp.zeros_like(target_ref)

    station = lax.broadcasted_iota(jnp.int32, (stations, rows), 0)
    touched = (station == one_ref[...]) | (station == two_ref[...])
    keep = keep_ref[0].astype(jnp.float32)
    vis = vis_ref[0].astype(jnp.float32)
    kept = touched & (keep > 0.0)
    plain = jnp.concatenate(
        [jnp.where(touched, vis[d : d + 1, :], 0.0) for d in range(directions)], axis=0
    ).astype(jnp.bfloat16)
    weighted = jnp.concatenate(
        [jnp.where(kept, vis[d : d + 1, :], 0.0) for d in range(directions)], axis=0
    ).astype(jnp.bfloat16)
    normal_ref[0] += lax.dot_general(
        weighted, plain, (NT, ((), ())), preferred_element_type=jnp.float32
    )
    data = obs_ref[0]
    high = data.astype(jnp.bfloat16).astype(jnp.float32)
    middle = (data - high).astype(jnp.bfloat16).astype(jnp.float32)
    low = data - high - middle
    pieces = jnp.concatenate([high, middle, low, jnp.zeros((5, rows), jnp.float32)], axis=0)
    target_ref[0] += lax.dot_general(
        pieces.astype(jnp.bfloat16), weighted, (NT, ((), ())), preferred_element_type=jnp.float32
    )


def normals(model_vis, observed, row_keep, station_one, station_two, padded):
    channels, directions, rows = model_vis.shape
    chunk = 1024 if rows % 1024 == 0 else rows
    return pl.pallas_call(
        normal_kernel,
        grid=(channels, rows // chunk),
        out_shape=[
            jax.ShapeDtypeStruct((channels, padded, padded), jnp.float32),
            jax.ShapeDtypeStruct((channels, 8, padded), jnp.float32),
        ],
        in_specs=[
            pl.BlockSpec((1, directions, chunk), lambda f, r: (f, 0, r)),
            pl.BlockSpec((1, 1, chunk), lambda f, r: (f, 0, r)),
            pl.BlockSpec((1, 1, chunk), lambda f, r: (f, 0, r)),
            pl.BlockSpec((1, chunk), lambda f, r: (0, r)),
            pl.BlockSpec((1, chunk), lambda f, r: (0, r)),
        ],
        out_specs=[
            pl.BlockSpec((1, padded, padded), lambda f, r: (f, 0, 0)),
            pl.BlockSpec((1, 8, padded), lambda f, r: (f, 0, 0)),
        ],
        compiler_params=pltpu.CompilerParams(vmem_limit_bytes=48 << 20),
    )(
        model_vis,
        observed.reshape(channels, 1, rows),
        row_keep.reshape(channels, 1, rows),
        station_one.reshape(1, rows),
        station_two.reshape(1, rows),
    )


def move(block, route):
    return lax.ppermute(block, "freq", route)


def body(model_vis, observed, row_keep, station_one, station_two, smoothness):
    channels, directions, _ = model_vis.shape
    assert channels == 2
    devices = lax.axis_size("freq")
    assert devices & (devices - 1) == 0
    position = lax.axis_index("freq")
    stations = smoothness.shape[0] // directions
    slots = -(-stations // 64) * 64
    width = directions * slots
    square, line = (width, width), (SUB, width)
    packed = (payload_rows(width), PANEL)
    smooth = jnp.pad(
        smoothness.reshape(directions, stations), ((0, 0), (0, slots - stations))
    ).reshape(width)

    normal, pieces = normals(model_vis, observed, row_keep, station_one, station_two, width)
    targets = jnp.sum(pieces, axis=1)
    identity = jnp.eye(width, dtype=jnp.float32)

    def diagonal(local):
        channel = position * channels + local
        neighbours = (
            2.0
            - (channel == 0).astype(jnp.float32)
            - (channel == channels * devices - 1).astype(jnp.float32)
        )
        return normal[local] + identity * (ridge_weight + neighbours * smooth)[:, None]

    def as_line(vector):
        return jnp.pad(vector[None, :], ((0, SUB - 1), (0, 0)))

    coupling, rise, y0, c, solved, inverse = call(
        first_kernel, (square, packed, line, (2,) + square, line, square),
        diagonal(0), as_line(targets[0]), smooth[None, :], scratch=(square,),
    )
    fall = move(rise, [(i, i - 1) for i in range(1, devices)])
    diag, source, below, above = diagonal(1), as_line(targets[1]), coupling, None

    levels = (devices - 1).bit_length()
    kept = []
    for level in range(levels):
        stride = 1 << level
        phase = lax.rem(position + 1, 4 * stride)
        mine = lax.rem(phase, 2 * stride) == stride
        drop = (phase == 3 * stride).astype(jnp.int32)
        flag = jnp.stack([mine.astype(jnp.int32), drop])
        sides = (below,) if level == 0 else (below, above)
        diag, source, up, down, cross, c, solved, inverse = call(
            functools.partial(level_kernel, level == 0),
            (square, line, packed, packed, square, (2,) + square, line, square),
            flag, diag, rise, fall, *sides, source, c, solved, inverse,
            scratch=(square, square, packed, packed, square),
            far_in=range(4, 4 + len(sides)),
            far_out=(2, 3, 4),
            sems=(pltpu.SemaphoreType.DMA((5,)),),
            aliases={1: 0, len(sides) + 4: 1, len(sides) + 5: 5, len(sides) + 6: 6, len(sides) + 7: 7},
        )
        kept.append(flag)
        gone = range(stride - 1, devices, 2 * stride)
        rises = [(i, i + stride) for i in gone]
        falls = [(i, i - stride) for i in gone if i >= stride]
        next_gone = range(2 * stride - 1, devices, 4 * stride) if level + 1 < levels else ()
        if next_gone:
            below = move(cross, [(i, j) for i, j in rises if j in next_gone])
            above = move(cross, [(i, j) for i, j in falls if j in next_gone])
        rise = move(up, rises)
        if falls:
            fall = move(down, falls)
    (gains,) = call(last_kernel, (line,), diag, rise, source, scratch=(square,))
    for level in reversed(range(levels)):
        stride = 1 << level
        flag = kept[level]
        gone = range(stride - 1, devices, 2 * stride)
        from_above = move(gains, [(i + stride, i) for i in gone])
        falling = [(i - stride, i) for i in gone if i >= stride]
        from_below = move(gains, falling) if falling else jnp.zeros_like(gains)
        (gains,) = call(back_kernel, (line,), flag, from_below, from_above, gains, c, solved, inverse)
    earlier = move(gains, [(i, i + 1) for i in range(devices - 1)])
    scale = jnp.where(smooth > 0, 1.0 / jnp.where(smooth > 0, smooth, 1.0), 0.0)
    first = y0 + mm(earlier + gains, coupling) * scale[None, :]
    both = jnp.stack([first[0], gains[0]])
    return both.reshape(channels, directions, slots)[:, :, :stations].reshape(
        channels, directions * stations
    )


def solution(mesh):
    placed = (P("freq", None, None), P("freq", None), P("freq", None), P(), P(), P())
    return jax.shard_map(
        body, mesh=mesh, in_specs=placed, out_specs=P("freq", None), check_vma=False
    )
```

```python
import functools

import jax
import jax.numpy as jnp
from jax import lax
from jax.experimental import pallas as pl
from jax.experimental.pallas import tpu as pltpu
from jax.sharding import PartitionSpec as P

ridge_weight = 1.0
PANEL = 128
SUB = 8
PIVOTS = 8
BLK = 32
VMEM_LIMIT = 24 << 20
HIGHEST = lax.Precision.HIGHEST


def mm(left, right, dims=((1,), (0,))):
    return lax.dot_general(
        left, right, (dims, ((), ())), precision=HIGHEST, preferred_element_type=jnp.float32
    )


NT = ((1,), (1,))
TN = ((0,), (0,))


def factor_panel(block):
    size = block.shape[0]
    strips = size // SUB
    lane = lax.broadcasted_iota(jnp.int32, (SUB, size), 1)
    sub = lax.broadcasted_iota(jnp.int32, (SUB, size), 0)
    index = range(PIVOTS)

    def spread(value):
        return jnp.broadcast_to(value, (SUB, size))

    def columns(value, k):
        return [jnp.take_along_axis(value, jnp.full((SUB, size), k + j, jnp.int32), axis=1) for j in index]

    a = [block[t * SUB : (t + 1) * SUB, :] for t in range(strips)]
    done = [jnp.zeros((SUB, size), jnp.float32) for _ in range(strips)]

    for k in range(0, size, PIVOTS):
        home, offset = k // SUB, k % SUB
        last = (k // BLK + 1) * BLK // SUB
        cols = columns(a[home], k)
        e = [[spread(cols[j][offset + i : offset + i + 1, :]) for j in range(i + 1)] for i in index]
        inverse, low = [], [[None] * PIVOTS for _ in index]
        for m in index:
            inverse.append(1.0 / e[m][m])
            for i in range(m + 1, PIVOTS):
                low[i][m] = e[i][m] * inverse[m]
                for j in range(m + 1, i + 1):
                    e[i][j] = e[i][j] - low[i][m] * e[j][m]
        inside = (lane >= k) & (lane < k + PIVOTS)
        u = []
        for i in index:
            row = spread(a[home][offset + i : offset + i + 1, :])
            value = jnp.where(inside, jnp.where(lane == k + i, 1.0, 0.0), row)
            for m in range(i):
                value = value - low[i][m] * u[m]
            u.append(value)
        s = [u[i] * inverse[i] for i in index]
        for i in reversed(index):
            for m in range(i + 1, PIVOTS):
                s[i] = s[i] - low[m][i] * s[m]
        for t in range((k + PIVOTS) // SUB, last):
            c = cols if t == home else columns(a[t], k)
            value = jnp.where(inside, 0.0, a[t])
            for j in index:
                value = value - c[j] * s[j]
            a[t] = value
        for i in index:
            root = lax.rsqrt(e[i][i])
            root = root * (1.5 - 0.5 * e[i][i] * root * root)
            done[home] = jnp.where(sub == offset + i, root * u[i], done[home])
        if offset + PIVOTS == SUB:
            keep = (lane <= sub + home * SUB) | (lane >= last * SUB)
            done[home] = jnp.where(keep, done[home], 0.0)
        if k + PIVOTS == last * SUB and last < strips:
            first = last - BLK // SUB
            rows = jnp.concatenate(done[first:last], axis=0)
            own = (lane >= first * SUB) & (lane < last * SUB)
            rest = jnp.concatenate([jnp.where(own, 0.0, a[t]) for t in range(last, strips)], axis=0)
            f = jnp.transpose(rows[:, last * SUB:])
            rest = rest - mm(f, rows)
            for t in range(last, strips):
                a[t] = rest[(t - last) * SUB : (t - last + 1) * SUB, :]
            for t in range(first, last):
                done[t] = jnp.where(lane < last * SUB, done[t], 0.0)
    return jnp.concatenate(done, axis=0)

def pairs(width):
    count = width // PANEL
    return [(r, c, r * (r + 1) // 2 + c) for r in range(count) for c in range(r + 1)]


def cut(index):
    return slice(index * PANEL, (index + 1) * PANEL)


def payload_rows(width):
    return len(pairs(width)) * PANEL + width // PANEL * SUB


def put_line(packed_ref, value):
    width = value.shape[1]
    base = len(pairs(width)) * PANEL
    for b in range(width // PANEL):
        packed_ref[base + b * SUB : base + (b + 1) * SUB, :] = value[:, cut(b)]


def get_line(packed_ref, width):
    base = len(pairs(width)) * PANEL
    return jnp.concatenate(
        [packed_ref[base + b * SUB : base + (b + 1) * SUB, :] for b in range(width // PANEL)], axis=1
    )


def fill_square(square_ref, packed_ref):
    for r, c, at in pairs(square_ref.shape[0]):
        piece = packed_ref[cut(at), :]
        square_ref[cut(r), cut(c)] = piece
        if r != c:
            square_ref[cut(c), cut(r)] = jnp.transpose(piece)


def factor(x_ref):
    width = x_ref.shape[0]
    count = width // PANEL

    @pl.loop(0, count)
    def _(step):
        own = pl.ds(pl.multiple_of(step * PANEL, PANEL), PANEL)
        x_ref[own, own] = factor_panel(x_ref[own, own])
        for p in range(count):

            @pl.when(step == p)
            def _():
                lo, hi = p * PANEL, (p + 1) * PANEL
                root = x_ref[lo:hi, lo:hi]
                if p:
                    x_ref[lo:hi, :lo] = mm(root, x_ref[lo:hi, :lo])
                if hi < width:
                    f = mm(x_ref[hi:, lo:hi], root, NT)
                    x_ref[hi:, hi:] = x_ref[hi:, hi:] - mm(f, f, NT)
                    if p:
                        x_ref[hi:, :lo] = x_ref[hi:, :lo] - mm(f, x_ref[lo:hi, :lo])
                    x_ref[hi:, lo:hi] = -mm(f, root)

    for r in range(count - 1):
        x_ref[cut(r), (r + 1) * PANEL :] = jnp.zeros((PANEL, width - (r + 1) * PANEL), jnp.float32)


def first_kernel(
    diag_ref, source_ref, across_ref, coupling_ref, packed_ref, y_ref, c_ref, line_ref, x_ref, t_ref
):
    width = diag_ref.shape[0]
    x_ref[...] = diag_ref[...]
    factor(x_ref)
    y = mm(mm(source_ref[...], x_ref[...], NT), x_ref[...])
    y_ref[...] = y
    put_line(packed_ref, y * across_ref[...])
    x_ref[...] = x_ref[...] * across_ref[...]
    for r, c, _ in pairs(width):
        t_ref[cut(c), cut(r)] = jnp.transpose(x_ref[cut(r), cut(c)])
    for r in range(width // PANEL):
        value = mm(t_ref[cut(r), r * PANEL :], x_ref[r * PANEL :, : (r + 1) * PANEL])
        for c in range(r + 1):
            packed_ref[cut(r * (r + 1) // 2 + c), :] = value[:, cut(c)]
    fill_square(coupling_ref, packed_ref)


def level_kernel(first, flag_ref, diag_ref, rise_ref, fall_ref, below_ref, *refs):
    if first:
        source_ref, _, _, _, *outs = refs
    else:
        above_ref, source_ref, _, _, _, *outs = refs
    diag_out, source_out, up_out, down_out, cross_out, c_ref, line_ref, x_ref, *holds = outs
    hold_ref, packed_ref, cross_ref, sems = holds
    width = diag_ref.shape[0]
    for r, c, at in pairs(width):
        diag_out[cut(r), cut(c)] = (
            diag_ref[cut(r), cut(c)] - rise_ref[cut(at), :] - fall_ref[cut(at), :]
        )
    source_out[...] = source_ref[...] + get_line(rise_ref, width) + get_line(fall_ref, width)

    @pl.when(flag_ref[0] == 1)
    def _():
        loads = [pltpu.make_async_copy(below_ref, hold_ref.at[0], sems.at[0])]
        if first:
            fill_square(hold_ref.at[1], fall_ref)
        else:
            loads.append(pltpu.make_async_copy(above_ref, hold_ref.at[1], sems.at[1]))
        for load in loads:
            load.start()
        x_ref[...] = diag_out[...]
        factor(x_ref)
        for load in loads:
            load.wait()
        half = width // 2

        @pl.loop(0, 2)
        def _(side):
            c_ref[side, :, :half] = mm(hold_ref[side, :, :half], x_ref[:half, :half], NT)
            c_ref[side, :, half:] = mm(hold_ref[side], x_ref[half:, :], NT)

        line = mm(source_out[...], x_ref[...], NT)
        line_ref[...] = line
        cross_ref[...] = mm(c_ref[flag_ref[1]], c_ref[1 - flag_ref[1]], NT)
        stores = [
            pltpu.make_async_copy(ref, out, sems.at[2 + i])
            for i, (ref, out) in enumerate(
                ((cross_ref, cross_out), (packed_ref.at[0], down_out), (packed_ref.at[1], up_out))
            )
        ]
        stores[0].start()

        @pl.loop(0, 2)
        def _(side):
            ref = packed_ref.at[side]
            put_line(ref, mm(line, c_ref[side], NT))
            for r in range(width // PANEL):
                value = mm(c_ref[side, cut(r), :], c_ref[side, : (r + 1) * PANEL, :], NT)
                for c in range(r + 1):
                    ref[cut(r * (r + 1) // 2 + c), :] = value[:, cut(c)]

        for store in stores[1:]:
            store.start()
        for store in stores:
            store.wait()


def last_kernel(diag_ref, rise_ref, source_ref, y_ref, x_ref):
    width = diag_ref.shape[0]
    for r, c, at in pairs(width):
        x_ref[cut(r), cut(c)] = diag_ref[cut(r), cut(c)] - rise_ref[cut(at), :]
    factor(x_ref)
    source = source_ref[...] + get_line(rise_ref, width)
    y_ref[...] = mm(mm(source, x_ref[...], NT), x_ref[...])


def back_kernel(flag_ref, below_ref, above_ref, gains_ref, c_ref, line_ref, x_ref, out_ref):
    out_ref[...] = gains_ref[...]

    @pl.when(flag_ref[0] == 1)
    def _():
        line = line_ref[...] + mm(below_ref[...], c_ref[0]) + mm(above_ref[...], c_ref[1])
        out_ref[...] = mm(line, x_ref[...])


def call(kernel, outs, *operands, scratch=(), aliases=None, far_in=(), far_out=(), sems=()):
    vmem = pl.BlockSpec(memory_space=pltpu.VMEM)
    smem = pl.BlockSpec(memory_space=pltpu.SMEM)
    far = pl.BlockSpec(memory_space=pl.ANY)
    return pl.pallas_call(
        kernel,
        out_shape=[jax.ShapeDtypeStruct(o, jnp.float32) for o in outs],
        in_specs=[
            smem if o.dtype == jnp.int32 else far if i in far_in else vmem
            for i, o in enumerate(operands)
        ],
        out_specs=[far if i in far_out else vmem for i in range(len(outs))],
        scratch_shapes=[pltpu.VMEM(s, jnp.float32) for s in scratch] + list(sems),
        input_output_aliases=aliases or {},
        compiler_params=pltpu.CompilerParams(vmem_limit_bytes=VMEM_LIMIT),
    )(*operands)

def normal_kernel(vis_ref, obs_ref, keep_ref, one_ref, two_ref, normal_ref, target_ref):
    padded = normal_ref.shape[1]
    directions, rows = vis_ref.shape[1], vis_ref.shape[2]
    stations = padded // directions

    @pl.when(pl.program_id(1) == 0)
    def _():
        normal_ref[...] = jnp.zeros_like(normal_ref)
        target_ref[...] = jnp.zeros_like(target_ref)

    station = lax.broadcasted_iota(jnp.int32, (stations, rows), 0)
    touched = (station == one_ref[...]) | (station == two_ref[...])
    own = pl.ds(pl.program_id(0), 1)
    keep = keep_ref[own, :].astype(jnp.float32)
    vis = vis_ref[0].astype(jnp.float32)
    kept = touched & (keep > 0.0)
    plain = jnp.concatenate(
        [jnp.where(touched, vis[d : d + 1, :], 0.0) for d in range(directions)], axis=0
    ).astype(jnp.bfloat16)
    weighted = jnp.concatenate(
        [jnp.where(kept, vis[d : d + 1, :], 0.0) for d in range(directions)], axis=0
    ).astype(jnp.bfloat16)
    normal_ref[0] += lax.dot_general(
        weighted, plain, (NT, ((), ())), preferred_element_type=jnp.float32
    )
    data = obs_ref[own, :]
    high = data.astype(jnp.bfloat16).astype(jnp.float32)
    middle = (data - high).astype(jnp.bfloat16).astype(jnp.float32)
    low = data - high - middle
    pieces = jnp.concatenate([high, middle, low, jnp.zeros((5, rows), jnp.float32)], axis=0)
    target_ref[0] += lax.dot_general(
        pieces.astype(jnp.bfloat16), weighted, (NT, ((), ())), preferred_element_type=jnp.float32
    )


def normals(model_vis, observed, row_keep, station_one, station_two, padded):
    channels, directions, rows = model_vis.shape
    chunk = 1024 if rows % 1024 == 0 else rows
    return pl.pallas_call(
        normal_kernel,
        grid=(channels, rows // chunk),
        out_shape=[
            jax.ShapeDtypeStruct((channels, padded, padded), jnp.float32),
            jax.ShapeDtypeStruct((channels, 8, padded), jnp.float32),
        ],
        in_specs=[
            pl.BlockSpec((1, directions, chunk), lambda f, r: (f, 0, r)),
            pl.BlockSpec((channels, chunk), lambda f, r: (0, r)),
            pl.BlockSpec((channels, chunk), lambda f, r: (0, r)),
            pl.BlockSpec((1, chunk), lambda f, r: (0, r)),
            pl.BlockSpec((1, chunk), lambda f, r: (0, r)),
        ],
        out_specs=[
            pl.BlockSpec((1, padded, padded), lambda f, r: (f, 0, 0)),
            pl.BlockSpec((1, 8, padded), lambda f, r: (f, 0, 0)),
        ],
        compiler_params=pltpu.CompilerParams(vmem_limit_bytes=48 << 20),
    )(
        model_vis,
        observed,
        row_keep,
        station_one.reshape(1, rows),
        station_two.reshape(1, rows),
    )


def move(block, route):
    return lax.ppermute(block, "freq", route)


def body(model_vis, observed, row_keep, station_one, station_two, smoothness):
    channels, directions, _ = model_vis.shape
    assert channels == 2
    devices = lax.axis_size("freq")
    assert devices & (devices - 1) == 0
    position = lax.axis_index("freq")
    stations = smoothness.shape[0] // directions
    slots = -(-stations // 64) * 64
    width = directions * slots
    square, line = (width, width), (SUB, width)
    packed = (payload_rows(width), PANEL)
    smooth = jnp.pad(
        smoothness.reshape(directions, stations), ((0, 0), (0, slots - stations))
    ).reshape(width)

    normal, pieces = normals(model_vis, observed, row_keep, station_one, station_two, width)
    targets = jnp.sum(pieces, axis=1)
    identity = jnp.eye(width, dtype=jnp.float32)

    def diagonal(local):
        channel = position * channels + local
        neighbours = (
            2.0
            - (channel == 0).astype(jnp.float32)
            - (channel == channels * devices - 1).astype(jnp.float32)
        )
        return normal[local] + identity * (ridge_weight + neighbours * smooth)[:, None]

    def as_line(vector):
        return jnp.pad(vector[None, :], ((0, SUB - 1), (0, 0)))

    coupling, rise, y0, c, solved, inverse = call(
        first_kernel, (square, packed, line, (2,) + square, line, square),
        diagonal(0), as_line(targets[0]), smooth[None, :], scratch=(square,),
    )
    fall = move(rise, [(i, i - 1) for i in range(1, devices)])
    diag, source, below, above = diagonal(1), as_line(targets[1]), coupling, None

    levels = (devices - 1).bit_length()
    kept = []
    for level in range(levels):
        stride = 1 << level
        phase = lax.rem(position + 1, 4 * stride)
        mine = lax.rem(phase, 2 * stride) == stride
        drop = (phase == 3 * stride).astype(jnp.int32)
        flag = jnp.stack([mine.astype(jnp.int32), drop])
        sides = (below,) if level == 0 else (below, above)
        diag, source, up, down, cross, c, solved, inverse = call(
            functools.partial(level_kernel, level == 0),
            (square, line, packed, packed, square, (2,) + square, line, square),
            flag, diag, rise, fall, *sides, source, c, solved, inverse,
            scratch=((2,) + square, (2,) + packed, square),
            far_in=range(4, 4 + len(sides)),
            far_out=(2, 3, 4),
            sems=(pltpu.SemaphoreType.DMA((5,)),),
            aliases={1: 0, len(sides) + 4: 1, len(sides) + 5: 5, len(sides) + 6: 6, len(sides) + 7: 7},
        )
        kept.append(flag)
        gone = range(stride - 1, devices, 2 * stride)
        rises = [(i, i + stride) for i in gone]
        falls = [(i, i - stride) for i in gone if i >= stride]
        next_gone = range(2 * stride - 1, devices, 4 * stride) if level + 1 < levels else ()
        if next_gone:
            below = move(cross, [(i, j) for i, j in rises if j in next_gone])
            above = move(cross, [(i, j) for i, j in falls if j in next_gone])
        rise = move(up, rises)
        if falls:
            fall = move(down, falls)
    (gains,) = call(last_kernel, (line,), diag, rise, source, scratch=(square,))
    for level in reversed(range(levels)):
        stride = 1 << level
        flag = kept[level]
        gone = range(stride - 1, devices, 2 * stride)
        from_above = move(gains, [(i + stride, i) for i in gone])
        falling = [(i - stride, i) for i in gone if i >= stride]
        from_below = move(gains, falling) if falling else jnp.zeros_like(gains)
        (gains,) = call(back_kernel, (line,), flag, from_below, from_above, gains, c, solved, inverse)
    earlier = move(gains, [(i, i + 1) for i in range(devices - 1)])
    scale = jnp.where(smooth > 0, 1.0 / jnp.where(smooth > 0, smooth, 1.0), 0.0)
    first = y0 + mm(earlier + gains, coupling) * scale[None, :]
    both = jnp.stack([first[0], gains[0]])
    return both.reshape(channels, directions, slots)[:, :, :stations].reshape(
        channels, directions * stations
    )


def solution(mesh):
    placed = (P("freq", None, None), P("freq", None), P("freq", None), P(), P(), P())
    return jax.shard_map(
        body, mesh=mesh, in_specs=placed, out_specs=P("freq", None), check_vma=False
    )
```
